32 devices in a mesh: fsdp: 8 (over z, x), rep: 4 (over y, core).
Axes of the slice: x: 2, y: 2, z: 4, core: 2. Of those that a mesh axis runs over, the one named last changes fastest.
Arguments:
- video_in: bfloat16 [32, 196, 1024], P(('fsdp', 'rep')), may hold values from -6 to 6
- audio_in: bfloat16 [32, 128, 1024], P(('fsdp', 'rep')), may hold values from -6 to 6
- bottle_in: bfloat16 [32, 8, 1024], P(('fsdp', 'rep')), may hold values from -6 to 6
- video_gain: float32 [1024], replicated, may hold values from 0.5 to 8
- audio_gain: float32 [1024], replicated, may hold values from 0.5 to 8
- video_qkv: bfloat16 [1024, 3072], P('fsdp'), may hold values from -0.18 to 0.18
- video_out: bfloat16 [1024, 1024], P('fsdp'), may hold values from -0.1875 to 0.1875
- audio_qkv: bfloat16 [1024, 3072], P('fsdp'), may hold values from -0.18 to 0.18
- audio_out: bfloat16 [1024, 1024], P('fsdp'), may hold values from -0.1875 to 0.1875
- grad_video: bfloat16 [32, 196, 1024], P(('fsdp', 'rep')), may hold values from -6 to 6
- grad_audio: bfloat16 [32, 128, 1024], P(('fsdp', 'rep')), may hold values from -6 to 6
- grad_bottle: bfloat16 [32, 8, 1024], P(('fsdp', 'rep')), may hold values from -6 to 6
Outputs:
- dvideo_in: bfloat16 [32, 196, 1024], P(('fsdp', 'rep'))
- daudio_in: bfloat16 [32, 128, 1024], P(('fsdp', 'rep'))
- dbottle_in: bfloat16 [32, 8, 1024], P(('fsdp', 'rep'))
- video_qkv_grad: float32 [1024, 3072], P('fsdp')
- video_out_grad: float32 [1024, 1024], P('fsdp')
- audio_qkv_grad: float32 [1024, 3072], P('fsdp')
- audio_out_grad: float32 [1024, 1024], P('fsdp')
- video_gain_grad: float32 [1024], replicated
- audio_gain_grad: float32 [1024], replicated
The draws below stay inside these ranges and needn't reach their ends.
All inputs are finite; a program needn't handle non-finite values.
Results may differ from the reference program's by a relative error of at most 0.025.
Values may be sent and summed in bfloat16 or wider, within the bound.
A program may use at most 128 MiB of HBM per device.

```python
import jax
import jax.numpy as jnp
from jax import lax

D = 1024
HEAD = 64
TV = 196
TA = 128
NB = 8
CPC = 1
CLIPS = 32


def gain_draw(key):
    return jax.random.uniform(key, (D,), jnp.float32, 0.5, 1.5)


def qkv_draw(key):
    base = jax.random.normal(key, (D, 3 * D), jnp.float32)
    return jnp.clip(base * D ** (-0.5), -0.18, 0.18).astype(jnp.bfloat16)


def draw_video_gain(key, part):
    return gain_draw(jax.random.fold_in(key, 101))


def draw_audio_gain(key, part):
    return gain_draw(jax.random.fold_in(key, 202))


def draw_video_qkv(key, part):
    return qkv_draw(jax.random.fold_in(key, 303))


def draw_audio_qkv(key, part):
    return qkv_draw(jax.random.fold_in(key, 404))


def level_of(key, dims, split, smallest, high):
    loudness = 1.0
    for axis_at, parts in split:
        draws = jax.random.uniform(jax.random.fold_in(jax.random.fold_in(key, 6), axis_at), (parts,), jnp.float32, smallest / len(split), high / len(split))
        loudness = loudness * jnp.repeat(jnp.exp(draws), dims[axis_at] // parts).reshape((-1,) + (1,) * (len(dims) - 1 - axis_at))
    return loudness


def bell_draw(rng, extent, spread, reach, pieces=(), dtype=jnp.bfloat16):
    factor_of = level_of(rng, extent, pieces, -0.22, 0.18) if pieces else 1.0
    entries = jax.random.normal(rng, extent, jnp.float32) * spread * factor_of
    return jnp.minimum(jnp.maximum(entries, -reach), reach).astype(dtype)


def setup_inputs(seed: int = 0) -> dict:
    keys = jax.random.split(jax.random.key(seed), 13)
    return {
        "video_in": bell_draw(keys[0], (CLIPS, TV, D), 1.0, 6.0, ((0, 32),)),
        "audio_in": bell_draw(keys[1], (CLIPS, TA, D), 1.0, 6.0, ((0, 32),)),
        "bottle_in": bell_draw(keys[2], (CLIPS, NB, D), 1.0, 6.0, ((0, 32),)),
        "video_gain": draw_video_gain(jax.random.fold_in(keys[12], 71), 0),
        "audio_gain": draw_audio_gain(jax.random.fold_in(keys[12], 71), 0),
        "video_qkv": draw_video_qkv(jax.random.fold_in(keys[12], 71), 0),
        "video_out": bell_draw(keys[6], (D, D), D ** -0.5, 0.1875, ((0, 8),)),
        "audio_qkv": draw_audio_qkv(jax.random.fold_in(keys[12], 71), 0),
        "audio_out": bell_draw(keys[8], (D, D), D ** -0.5, 0.1875, ((0, 8),)),
        "grad_video": bell_draw(keys[9], (CLIPS, TV, D), 1.0, 6.0, ((0, 32),)),
        "grad_audio": bell_draw(keys[10], (CLIPS, TA, D), 1.0, 6.0, ((0, 32),)),
        "grad_bottle": bell_draw(keys[11], (CLIPS, NB, D), 1.0, 6.0, ((0, 32),)),
    }


def stream(tokens, bottle, gain, w_qkv, w_out, d_tokens, bottle_half):
    f32 = jnp.float32
    bf16 = jnp.bfloat16
    z_rows = jnp.concatenate([tokens, bottle], 0)
    rows = z_rows.shape[0]
    width = z_rows.shape[1]
    zf = z_rows.astype(f32)
    inverse = lax.rsqrt(lax.optimization_barrier(jnp.mean(zf * zf, axis=1, keepdims=True)) + 1e-06)
    normed = zf * inverse
    hidden = (normed * gain).astype(bf16)
    qkv = jnp.dot(hidden, w_qkv, preferred_element_type=f32).astype(bf16)
    scale = HEAD ** (-0.5)
    query = qkv[:, :width].reshape(rows, -1, HEAD).astype(f32)
    keyed = qkv[:, width:2 * width].reshape(rows, -1, HEAD).astype(f32)
    valued = qkv[:, 2 * width:].reshape(rows, -1, HEAD).astype(f32)
    scores = jnp.einsum('shd,thd->hst', query, keyed) * scale
    probs = jax.nn.softmax(scores, axis=-1)
    pb = probs.astype(bf16).astype(f32)
    att = jnp.einsum('hst,thd->shd', pb, valued).reshape(rows, width).astype(bf16)
    d_out = jnp.concatenate([d_tokens.astype(f32), bottle_half], 0)
    dyb = d_out.astype(bf16)
    out_term = jnp.dot(att.T, dyb, preferred_element_type=f32)
    datt = jnp.dot(dyb, w_out.T, preferred_element_type=f32).astype(bf16)
    datt_f = datt.reshape(rows, -1, HEAD).astype(f32)
    dprob = jnp.einsum('shd,thd->hst', datt_f, valued)
    dvalue = jnp.einsum('hst,shd->thd', pb, datt_f)
    dscore = probs * (dprob - lax.optimization_barrier(jnp.sum(probs * dprob, axis=-1, keepdims=True))) * scale
    dsb = dscore.astype(bf16).astype(f32)
    dquery = jnp.einsum('hst,thd->shd', dsb, keyed)
    dkey = jnp.einsum('hst,shd->thd', dsb, query)
    dqkv = jnp.concatenate([dquery.reshape(rows, width), dkey.reshape(rows, width), dvalue.reshape(rows, width)], 1).astype(bf16)
    qkv_term = jnp.dot(hidden.T, dqkv, preferred_element_type=f32)
    dhidden = jnp.dot(dqkv, w_qkv.T, preferred_element_type=f32)
    gain_term = lax.optimization_barrier(jnp.sum(dhidden * normed, axis=0))
    dnorm = dhidden * gain
    d_z = d_out + inverse * (dnorm - normed * lax.optimization_barrier(jnp.mean(dnorm * normed, axis=1, keepdims=True)))
    return (d_z, qkv_term, out_term, gain_term)

def rounded(term):
    return lax.optimization_barrier(term.astype(jnp.bfloat16)).astype(jnp.float32)

def reference(video_in, audio_in, bottle_in, video_gain, audio_gain, video_qkv, video_out, audio_qkv, audio_out, grad_video, grad_audio, grad_bottle):

    def one_clip(carry, item):
        x_video, x_audio, x_bottle, g_video, g_audio, g_bottle = item
        half = g_bottle.astype(jnp.float32) * 0.5
        dz_video, qv, ov, gv = stream(x_video, x_bottle, video_gain, video_qkv, video_out, g_video, half)
        dz_audio, qa, oa, ga = stream(x_audio, x_bottle, audio_gain, audio_qkv, audio_out, g_audio, half)
        carry = (carry[0] + qv, carry[1] + ov, carry[2] + qa, carry[3] + oa, carry[4] + gv, carry[5] + ga)
        outs = (dz_video[:TV].astype(jnp.bfloat16), dz_audio[:TA].astype(jnp.bfloat16), (dz_video[TV:] + dz_audio[TA:]).astype(jnp.bfloat16))
        return (carry, outs)

    def zeros_all():
        return (jnp.zeros((D, 3 * D), jnp.float32), jnp.zeros((D, D), jnp.float32), jnp.zeros((D, 3 * D), jnp.float32), jnp.zeros((D, D), jnp.float32), jnp.zeros((D,), jnp.float32), jnp.zeros((D,), jnp.float32))

    def one_device(carry, group):
        local, outs = lax.scan(one_clip, zeros_all(), group)
        carry = (carry[0] + rounded(local[0]), carry[1] + rounded(local[1]), carry[2] + rounded(local[2]), carry[3] + rounded(local[3]), carry[4] + local[4], carry[5] + local[5])
        return (carry, outs)
    groups = CLIPS // CPC
    items = (video_in, audio_in, bottle_in, grad_video, grad_audio, grad_bottle)
    items = tuple((a.reshape((groups, CPC) + a.shape[1:]) for a in items))
    sums, outs = lax.scan(one_device, zeros_all(), items)
    count = float(CLIPS)
    dv = outs[0].reshape(CLIPS, TV, D)
    da = outs[1].reshape(CLIPS, TA, D)
    db = outs[2].reshape(CLIPS, NB, D)
    return (dv, da, db, sums[0] / count, sums[1] / count, sums[2] / count, sums[3] / count, sums[4] / count, sums[5] / count)
```

```python
import functools

import jax
import jax.numpy as jnp
from jax import lax
from jax.experimental import pallas as pl
from jax.experimental.pallas import tpu as pltpu
from jax.sharding import PartitionSpec as P

HEAD = 64
f32 = jnp.float32
bf16 = jnp.bfloat16


def remote(src, dst, send, recv, f, r):
    return pltpu.make_async_remote_copy(
        src_ref=src,
        dst_ref=dst,
        send_sem=send,
        recv_sem=recv,
        device_id={"fsdp": f, "rep": r},
        device_id_type=pl.DeviceIdType.MESH,
    )


def places(n, R):
    f = lax.axis_index("fsdp")
    r = lax.axis_index("rep")
    line = f // 2
    x = lax.rem(f, 2)
    return f, r, line, x, f + 1 - 2 * x


def greet(n, R):
    f, r, line, x, partner = places(n, R)
    barrier = pltpu.get_barrier_semaphore()

    def signal(ff, rr):
        pl.semaphore_signal(
            barrier,
            inc=1,
            device_id={"fsdp": ff, "rep": rr},
            device_id_type=pl.DeviceIdType.MESH,
        )

    signal(partner, r)
    for j in range(1, n // 2):
        signal(lax.rem(line + j, n // 2) * 2 + x, r)
    for j in range(1, R):
        signal(f, lax.rem(r + j, R))
    pl.semaphore_wait(barrier, n // 2 + R - 1)


def gather_kernel(n, R, oc, w_ref, tv_ref, ta_ref, wf, wo, gv, ga, zs, zr, xs, xr, ts, tr, os, orr, loc):
    L = n // 2
    G = n // R
    H = R // 2
    f, r, line, x, partner = places(n, R)
    mate = r + 1 - 2 * lax.rem(r, 2)
    greet(n, R)
    C = w_ref.shape[2]

    own = [pltpu.make_async_copy(w_ref.at[s], wf.at[s, f], loc.at[s]) for s in range(2)]
    own_t = [
        pltpu.make_async_copy(tv_ref, gv.at[r], loc.at[2]),
        pltpu.make_async_copy(ta_ref, ga.at[r], loc.at[3]),
    ]
    along = []
    across = []
    tokens = []
    relay = []
    for s in range(2):
        row = []
        for j in range(1, L):
            c = remote(w_ref.at[s], wf.at[s, f], zs.at[s, j], zr.at[s, j], lax.rem(line + j, L) * 2 + x, r)
            c.start()
            row.append(c)
        along.append(row)
        c = remote(w_ref.at[s], wf.at[s, f], xs.at[s, 0], xr.at[s, 0], partner, r)
        c.start()
        across.append([c])
        src, dst = (tv_ref, gv) if s == 0 else (ta_ref, ga)
        row = []
        for j in range(1, H):
            c = remote(src, dst.at[r], ts.at[s, j], tr.at[s, j], f, lax.rem(r + 2 * j, R))
            c.start()
            row.append(c)
        tokens.append(row)
        c = remote(src, dst.at[r], ts.at[s, 0], tr.at[s, 0], f, mate)
        c.start()
        relay.append([c])
    for c in own + own_t:
        c.start()
    for s in range(2):
        dst = gv if s == 0 else ga
        for j in range(1, L):
            along[s][j - 1].wait_recv()
            b = lax.rem(line - j + L, L) * 2 + x
            c = remote(wf.at[s, b], wf.at[s, b], xs.at[s, j], xr.at[s, j], partner, r)
            c.start()
            across[s].append(c)
        for j in range(1, H):
            tokens[s][j - 1].wait_recv()
            b = lax.rem(r - 2 * j + R, R)
            c = remote(dst.at[b], dst.at[b], ts.at[s, H - 1 + j], tr.at[s, H - 1 + j], f, mate)
            c.start()
            relay[s].append(c)
    swap = []
    for s in range(2):
        own[s].wait()
        for c in across[s]:
            c.wait_recv()
        for j in range(1, R):
            p = lax.rem(r + j, R)
            c = remote(
                wf.at[s, pl.ds(p * G, G), :, pl.ds(C - oc, oc)],
                wo.at[s, r],
                os.at[s, j],
                orr.at[s, j],
                f,
                p,
            )
            c.start()
            swap.append(c)
        c = pltpu.make_async_copy(
            wf.at[s, pl.ds(r * G, G), :, pl.ds(C - oc, oc)], wo.at[s, r], loc.at[4 + s]
        )
        c.start()
        own_t.append(c)
    for c in own_t:
        c.wait()
    for s in range(2):
        for c in along[s] + across[s] + tokens[s] + relay[s]:
            c.wait_send()
        for c in relay[s]:
            c.wait_recv()
    for c in swap:
        c.wait()


def gather(n, R, oc, w, tv, ta):
    _, rows, C = w.shape
    H = R // 2
    G = n // R
    dma = pltpu.SemaphoreType.DMA
    vm = pl.BlockSpec(memory_space=pltpu.VMEM)
    return pl.pallas_call(
        functools.partial(gather_kernel, n, R, oc),
        out_shape=(
            jax.ShapeDtypeStruct((2, n, rows, C), bf16),
            jax.ShapeDtypeStruct((2, R, G, rows, oc), bf16),
            jax.ShapeDtypeStruct((R,) + tv.shape, bf16),
            jax.ShapeDtypeStruct((R,) + ta.shape, bf16),
        ),
        in_specs=[vm] * 3,
        out_specs=(vm,) * 4,
        scratch_shapes=[
            dma((2, n // 2)),
            dma((2, n // 2)),
            dma((2, n // 2)),
            dma((2, n // 2)),
            dma((2, 2 * H)),
            dma((2, 2 * H)),
            dma((2, R)),
            dma((2, R)),
            dma((6,)),
        ],
        compiler_params=pltpu.CompilerParams(
            collective_id=0, has_side_effects=True, vmem_limit_bytes=60 * 1024 * 1024
        ),
    )(w, tv, ta)


def reduce_kernel(n, R, oc, gq, go, dv, da, gain, fin, rv, ra, gsum,
                  ob, xq, xo, sq, so, zq, zo, fb, gx, gb, gc,
                  as_, ar, qs, qr, ps, pr, us, ur, vs, vr, es, er, ds_, dr, ks, kr, loc):
    L = n // 2
    G = n // R
    f, r, line, x, partner = places(n, R)
    C3 = gq.shape[3]
    greet(n, R)
    done = []
    turn = []
    own = []
    for s in range(2):
        row = []
        for j in range(1, R):
            p = lax.rem(r + j, R)
            c = remote(
                go.at[s, :, :, pl.ds(pl.multiple_of(p * oc, oc), oc)],
                ob.at[s, pl.ds(r * G, G)],
                as_.at[s, j],
                ar.at[s, j],
                f,
                p,
            )
            c.start()
            row.append(c)
        turn.append(row)
        c = pltpu.make_async_copy(
            go.at[s, :, :, pl.ds(pl.multiple_of(r * oc, oc), oc)],
            ob.at[s, pl.ds(r * G, G)],
            loc.at[s],
        )
        c.start()
        own.append(c)
    cg = remote(gain, gx, ks.at[0], kr.at[0], partner, r)
    cg.start()
    cross_q = []
    for s in range(2):
        row = []
        for k in range(L):
            j = lax.rem(line + k, L)
            c = remote(gq.at[s, 2 * j + 1 - x], xq.at[s, j], qs.at[s, k], qr.at[s, k], partner, r)
            c.start()
            row.append(c)
        cross_q.append(row)
    back = []
    for s, (src, dst) in enumerate(((dv, rv), (da, ra))):
        for j in range(1, R):
            p = lax.rem(r + j, R)
            c = remote(src.at[p], dst.at[j - 1], ds_.at[s, j], dr.at[s, j], f, p)
            c.start()
            back.append(c)
    cg.wait_recv()
    gb[line] = gain[...] + gx[...]
    line_g = []
    for j in range(1, L):
        c = remote(gb.at[line], gb.at[line], ks.at[j], kr.at[j], lax.rem(line + j, L) * 2 + x, r)
        c.start()
        line_g.append(c)
    cross_o = []
    for s in range(2):
        own[s].wait()
        for c in turn[s]:
            c.wait_recv()
        row = []
        for k in range(L):
            j = lax.rem(line + k, L)
            c = remote(ob.at[s, 2 * j + 1 - x], xo.at[s, j], ps.at[s, k], pr.at[s, k], partner, r)
            c.start()
            row.append(c)
        cross_o.append(row)
    for c in line_g:
        c.wait_recv()
    total = gb[0]
    for j in range(1, L):
        total = total + gb[j]
    gc[r] = total
    group_g = []
    for j in range(1, R):
        c = remote(gc.at[r], gc.at[r], ks.at[L + j], kr.at[L + j], f, lax.rem(r + j, R))
        c.start()
        group_g.append(c)
    along_q = []
    along_o = []
    for s in range(2):
        row_q = []
        row_o = []
        for k in list(range(1, L)) + [0]:
            j = lax.rem(line + k, L)
            cross_q[s][k].wait_recv()
            sq[s, j] = (gq[s, 2 * j + x].astype(f32) + xq[s, j].astype(f32)).astype(bf16)
            if k:
                c = remote(sq.at[s, j], zq.at[s, k - 1], us.at[s, k], ur.at[s, k], 2 * j + x, r)
                c.start()
                row_q.append(c)
            cross_o[s][k].wait_recv()
            so[s, j] = (ob[s, 2 * j + x].astype(f32) + xo[s, j].astype(f32)).astype(bf16)
            if k:
                c = remote(so.at[s, j], zo.at[s, k - 1], vs.at[s, k], vr.at[s, k], 2 * j + x, r)
                c.start()
                row_o.append(c)
        along_q.append(row_q)
        along_o.append(row_o)
    spread = []
    for s in range(2):
        tq = sq[s, line].astype(f32)
        to = so[s, line].astype(f32)
        for k in range(1, L):
            along_q[s][k - 1].wait_recv()
            tq = tq + zq[s, k - 1].astype(f32)
            along_o[s][k - 1].wait_recv()
            to = to + zo[s, k - 1].astype(f32)
        fb[s, :, pl.ds(0, C3)] = tq.astype(bf16)
        fb[s, :, pl.ds(C3, oc)] = to.astype(bf16)
        fin[s, r, :, pl.ds(0, C3)] = tq.astype(bf16)
        fin[s, r, :, pl.ds(C3, oc)] = to.astype(bf16)
        for j in range(1, R):
            c = remote(fb.at[s], fin.at[s, r], es.at[s, j], er.at[s, j], f, lax.rem(r + j, R))
            c.start()
            spread.append(c)
    for c in group_g:
        c.wait_recv()
    total = gc[0]
    for j in range(1, R):
        total = total + gc[j]
    gsum[...] = total
    for c in back + spread:
        c.wait()
    for c in [cg] + line_g + group_g:
        c.wait_send()
    for s in range(2):
        for c in turn[s] + cross_q[s] + cross_o[s] + along_q[s] + along_o[s]:
            c.wait_send()


def reduce_all(n, R, oc, gq, go, dv, da, gain):
    _, _, rows, C3 = gq.shape
    L = n // 2
    C = C3 + oc
    dma = pltpu.SemaphoreType.DMA
    vm = pl.BlockSpec(memory_space=pltpu.VMEM)
    V = pltpu.VMEM
    return pl.pallas_call(
        functools.partial(reduce_kernel, n, R, oc),
        out_shape=(
            jax.ShapeDtypeStruct((2, R, rows, C), bf16),
            jax.ShapeDtypeStruct((R - 1,) + dv.shape[1:], bf16),
            jax.ShapeDtypeStruct((R - 1,) + da.shape[1:], bf16),
            jax.ShapeDtypeStruct(gain.shape, f32),
        ),
        in_specs=[vm] * 5,
        out_specs=(vm,) * 4,
        scratch_shapes=[
            V((2, n, rows, oc), bf16),
            V((2, L, rows, C3), bf16),
            V((2, L, rows, oc), bf16),
            V((2, L, rows, C3), bf16),
            V((2, L, rows, oc), bf16),
            V((2, L - 1, rows, C3), bf16),
            V((2, L - 1, rows, oc), bf16),
            V((2, rows, C), bf16),
            V(gain.shape, f32),
            V((L,) + gain.shape, f32),
            V((R,) + gain.shape, f32),
            dma((2, R)),
            dma((2, R)),
            dma((2, L)),
            dma((2, L)),
            dma((2, L)),
            dma((2, L)),
            dma((2, L)),
            dma((2, L)),
            dma((2, L)),
            dma((2, L)),
            dma((2, R)),
            dma((2, R)),
            dma((2, R)),
            dma((2, R)),
            dma((L + R,)),
            dma((L + R,)),
            dma((2,)),
        ],
        compiler_params=pltpu.CompilerParams(
            collective_id=1, has_side_effects=True, vmem_limit_bytes=60 * 1024 * 1024
        ),
    )(gq, go, dv, da, gain)


def normalise(z):
    zf = z.astype(f32)
    inverse = lax.rsqrt(jnp.mean(zf * zf, axis=-1, keepdims=True) + 1e-06)
    return zf * inverse, inverse


def stream(z, dyb, gain, w, wo, length):
    clips, rows, width = z.shape
    cols = w.shape[1] // 3
    normed, _ = normalise(z)
    hidden = (normed * gain).astype(bf16)
    qkv = jnp.einsum("csd,de->cse", hidden, w, preferred_element_type=f32).astype(bf16)
    scale = HEAD ** (-0.5)
    query = qkv[..., :cols].reshape(clips, rows, -1, HEAD)
    keyed = qkv[..., cols : 2 * cols].reshape(clips, rows, -1, HEAD)
    valued = qkv[..., 2 * cols :].reshape(clips, rows, -1, HEAD)
    scores = jnp.einsum("cshd,cthd->chst", query, keyed, preferred_element_type=f32) * scale
    real = lax.broadcasted_iota(jnp.int32, scores.shape, 3) < length
    probs = jax.nn.softmax(jnp.where(real, scores, -1e30), axis=-1)
    pb = probs.astype(bf16)
    att = (
        jnp.einsum("chst,cthd->cshd", pb, valued, preferred_element_type=f32)
        .reshape(clips, rows, cols)
        .astype(bf16)
    )
    out_term = jnp.einsum("csd,cse->de", att, dyb, preferred_element_type=f32).astype(bf16)
    datt = jnp.einsum("cse,de->csd", dyb, wo, preferred_element_type=f32).astype(bf16)
    datt = datt.reshape(clips, rows, -1, HEAD)
    dprob = jnp.einsum("cshd,cthd->chst", datt, valued, preferred_element_type=f32)
    dvalue = jnp.einsum("chst,cshd->cthd", pb, datt, preferred_element_type=f32)
    dscore = probs * (dprob - jnp.sum(probs * dprob, axis=-1, keepdims=True)) * scale
    dsb = dscore.astype(bf16)
    dquery = jnp.einsum("chst,cthd->cshd", dsb, keyed, preferred_element_type=f32)
    dkey = jnp.einsum("chst,cshd->cthd", dsb, query, preferred_element_type=f32)
    dqkv = jnp.concatenate(
        [t.astype(bf16).reshape(clips, rows, cols) for t in (dquery, dkey, dvalue)], 2
    )
    qkv_term = jnp.einsum("csd,cse->de", hidden, dqkv, preferred_element_type=f32).astype(bf16)
    dhidden = jnp.einsum("cse,de->csd", dqkv, w, preferred_element_type=f32)
    gain_term = jnp.sum(dhidden * normed, axis=(0, 1))
    return qkv_term, out_term, dhidden.astype(bf16), gain_term


def d_rows(z, d_out, dh, gain):
    normed, inverse = normalise(z)
    dnorm = dh * gain
    return d_out + inverse * (dnorm - normed * jnp.mean(dnorm * normed, axis=-1, keepdims=True))


def padded(tokens, bottle):
    rows = tokens.shape[1] + bottle.shape[1]
    return jnp.pad(jnp.concatenate([tokens, bottle], 1), ((0, 0), (0, -rows % 16), (0, 0)))


def per_device(
    n,
    R,
    video_in,
    audio_in,
    bottle_in,
    video_gain,
    audio_gain,
    video_qkv,
    video_out,
    audio_qkv,
    audio_out,
    grad_video,
    grad_audio,
    grad_bottle,
):
    r = lax.axis_index("rep")
    clips = video_in.shape[0]
    count = float(clips * n * R)
    rows, width = video_out.shape
    oc = width // R

    def quarter(qkv, out):
        parts = [lax.dynamic_slice_in_dim(qkv, k * width + r * oc, oc, 1) for k in range(3)]
        return jnp.concatenate(parts + [lax.dynamic_slice_in_dim(out, r * oc, oc, 1)], 1)

    w = jnp.stack([quarter(video_qkv, video_out), quarter(audio_qkv, audio_out)])
    half = (grad_bottle.astype(f32) * 0.5).astype(bf16)
    zs = [padded(video_in, bottle_in), padded(audio_in, bottle_in)]
    dys = [padded(grad_video, half), padded(grad_audio, half)]
    tv, ta = [jnp.stack([z, dy]) for z, dy in zip(zs, dys)]
    wf, wo, gv, ga = gather(n, R, oc, w, tv, ta)

    lengths = [t.shape[1] + bottle_in.shape[1] for t in (video_in, audio_in)]
    gains = [video_gain, audio_gain]
    results = []
    for s, got in enumerate((gv, ga)):
        full = wf[s].reshape(n * rows, -1)[:, : 3 * oc]
        rows_out = jnp.moveaxis(wo[s].reshape(R, oc, oc), 0, 1).reshape(oc, width)
        p = got.shape[3]
        z = got[:, 0].reshape(R * clips, p, width)
        dy = got[:, 1].reshape(R * clips, p, width)
        results.append(stream(z, dy, gains[s], full, rows_out, lengths[s]))
    gq = jnp.stack([res[0].reshape(n, rows, 3 * oc) for res in results])
    go = jnp.stack([res[1].reshape(n // R, rows, width) for res in results])
    dhs = [res[2].reshape((R, clips) + res[2].shape[1:]) for res in results]
    gain_terms = jnp.stack([res[3] for res in results])
    fin, rv, ra, gsum = reduce_all(n, R, oc, gq, go, dhs[0], dhs[1], gain_terms)
    gsum = gsum / count

    dzs = []
    for s, got in enumerate((rv, ra)):
        dh = lax.dynamic_index_in_dim(dhs[s], r, 0, keepdims=False).astype(f32)
        for j in range(R - 1):
            dh = dh + got[j].astype(f32)
        dzs.append(d_rows(zs[s], dys[s].astype(f32), dh, gains[s]))
    grads = []
    for s in range(2):
        q = jnp.moveaxis(fin[s, :, :, : 3 * oc].reshape(R, rows, 3, oc), 0, 2)
        grads.append(q.reshape(rows, 3 * width).astype(f32) / count)
        o = jnp.moveaxis(fin[s, :, :, 3 * oc :], 0, 1)
        grads.append(o.reshape(rows, width).astype(f32) / count)
    tv_len, ta_len = video_in.shape[1], audio_in.shape[1]
    dbottle = dzs[0][:, tv_len : lengths[0]] + dzs[1][:, ta_len : lengths[1]]
    return (
        dzs[0][:, :tv_len].astype(bf16),
        dzs[1][:, :ta_len].astype(bf16),
        dbottle.astype(bf16),
        grads[0],
        grads[1],
        grads[2],
        grads[3],
        gsum[0],
        gsum[1],
    )


def solution(mesh):
    n = mesh.shape["fsdp"]
    R = mesh.shape["rep"]
    clip = P(("fsdp", "rep"), None, None)
    shard = P("fsdp", None)
    in_specs = (clip, clip, clip, P(), P(), shard, shard, shard, shard, clip, clip, clip)
    out_specs = (clip, clip, clip, shard, shard, shard, shard, P(), P())
    return jax.shard_map(
        functools.partial(per_device, n, R),
        mesh=mesh,
        in_specs=in_specs,
        out_specs=out_specs,
        check_vma=False,
    )
```

```python
import functools

import jax
import jax.numpy as jnp
from jax import lax
from jax.experimental import pallas as pl
from jax.experimental.pallas import tpu as pltpu
from jax.sharding import PartitionSpec as P

HEAD = 64
f32 = jnp.float32
bf16 = jnp.bfloat16


def remote(src, dst, send, recv, f, r):
    return pltpu.make_async_remote_copy(
        src_ref=src,
        dst_ref=dst,
        send_sem=send,
        recv_sem=recv,
        device_id={"fsdp": f, "rep": r},
        device_id_type=pl.DeviceIdType.MESH,
    )


def places(n, R):
    f = lax.axis_index("fsdp")
    r = lax.axis_index("rep")
    line = f // 2
    x = lax.rem(f, 2)
    return f, r, line, x, f + 1 - 2 * x


def greet(n, R):
    f, r, line, x, partner = places(n, R)
    barrier = pltpu.get_barrier_semaphore()

    def signal(ff, rr):
        pl.semaphore_signal(
            barrier,
            inc=1,
            device_id={"fsdp": ff, "rep": rr},
            device_id_type=pl.DeviceIdType.MESH,
        )

    signal(partner, r)
    for j in range(1, n // 2):
        signal(lax.rem(line + j, n // 2) * 2 + x, r)
    for j in range(1, R):
        signal(f, lax.rem(r + j, R))
    pl.semaphore_wait(barrier, n // 2 + R - 1)


def gather_kernel(n, R, oc, w_ref, tv_ref, ta_ref, wf, wo, gv, ga, zs, zr, xs, xr, ts, tr, os, orr, loc):
    L = n // 2
    G = n // R
    H = R // 2
    f, r, line, x, partner = places(n, R)
    mate = r + 1 - 2 * lax.rem(r, 2)
    greet(n, R)
    C = w_ref.shape[2]

    own = [pltpu.make_async_copy(w_ref.at[s], wf.at[s, f], loc.at[s]) for s in range(2)]
    own_t = [
        pltpu.make_async_copy(tv_ref, gv.at[r], loc.at[2]),
        pltpu.make_async_copy(ta_ref, ga.at[r], loc.at[3]),
    ]
    along = []
    across = []
    tokens = []
    relay = []
    for s in range(2):
        row = []
        for j in range(1, L):
            c = remote(w_ref.at[s], wf.at[s, f], zs.at[s, j], zr.at[s, j], lax.rem(line + j, L) * 2 + x, r)
            c.start()
            row.append(c)
        along.append(row)
        c = remote(w_ref.at[s], wf.at[s, f], xs.at[s, 0], xr.at[s, 0], partner, r)
        c.start()
        across.append([c])
        src, dst = (tv_ref, gv) if s == 0 else (ta_ref, ga)
        row = []
        for j in range(1, H):
            c = remote(src, dst.at[r], ts.at[s, j], tr.at[s, j], f, lax.rem(r + 2 * j, R))
            c.start()
            row.append(c)
        tokens.append(row)
        c = remote(src, dst.at[r], ts.at[s, 0], tr.at[s, 0], f, mate)
        c.start()
        relay.append([c])
    for c in own + own_t:
        c.start()
    for s in range(2):
        dst = gv if s == 0 else ga
        for j in range(1, L):
            along[s][j - 1].wait_recv()
            b = lax.rem(line - j + L, L) * 2 + x
            c = remote(wf.at[s, b], wf.at[s, b], xs.at[s, j], xr.at[s, j], partner, r)
            c.start()
            across[s].append(c)
        for j in range(1, H):
            tokens[s][j - 1].wait_recv()
            b = lax.rem(r - 2 * j + R, R)
            c = remote(dst.at[b], dst.at[b], ts.at[s, H - 1 + j], tr.at[s, H - 1 + j], f, mate)
            c.start()
            relay[s].append(c)
    swap = []
    for s in range(2):
        own[s].wait()
        for c in across[s]:
            c.wait_recv()
        for j in range(1, R):
            p = lax.rem(r + j, R)
            c = remote(
                wf.at[s, pl.ds(p * G, G), :, pl.ds(C - oc, oc)],
                wo.at[s, r],
                os.at[s, j],
                orr.at[s, j],
                f,
                p,
            )
            c.start()
            swap.append(c)
        c = pltpu.make_async_copy(
            wf.at[s, pl.ds(r * G, G), :, pl.ds(C - oc, oc)], wo.at[s, r], loc.at[4 + s]
        )
        c.start()
        own_t.append(c)
    for c in own_t:
        c.wait()
    for s in range(2):
        for c in along[s] + across[s] + tokens[s] + relay[s]:
            c.wait_send()
        for c in relay[s]:
            c.wait_recv()
    for c in swap:
        c.wait()


def gather(n, R, oc, w, tv, ta):
    _, rows, C = w.shape
    H = R // 2
    G = n // R
    dma = pltpu.SemaphoreType.DMA
    vm = pl.BlockSpec(memory_space=pltpu.VMEM)
    return pl.pallas_call(
        functools.partial(gather_kernel, n, R, oc),
        out_shape=(
            jax.ShapeDtypeStruct((2, n, rows, C), bf16),
            jax.ShapeDtypeStruct((2, R, G, rows, oc), bf16),
            jax.ShapeDtypeStruct((R,) + tv.shape, bf16),
            jax.ShapeDtypeStruct((R,) + ta.shape, bf16),
        ),
        in_specs=[vm] * 3,
        out_specs=(vm,) * 4,
        scratch_shapes=[
            dma((2, n // 2)),
            dma((2, n // 2)),
            dma((2, n // 2)),
            dma((2, n // 2)),
            dma((2, 2 * H)),
            dma((2, 2 * H)),
            dma((2, R)),
            dma((2, R)),
            dma((6,)),
        ],
        compiler_params=pltpu.CompilerParams(
            collective_id=0, has_side_effects=True, vmem_limit_bytes=60 * 1024 * 1024
        ),
    )(w, tv, ta)


def reduce_kernel(n, R, oc, gq, go, dv, da, gain, fin, rv, ra, gsum,
                  ob, xq, xo, sq, so, zq, zo, fb, gx, gb, gc,
                  as_, ar, qs, qr, ps, pr, us, ur, vs, vr, es, er, ds_, dr, ks, kr, loc):
    L = n // 2
    G = n // R
    f, r, line, x, partner = places(n, R)
    C3 = gq.shape[3]
    H = R // 2
    mate = r + 1 - 2 * lax.rem(r, 2)
    greet(n, R)
    done = []
    turn = []
    own = []
    for s in range(2):
        row = []
        for j in range(1, R):
            p = lax.rem(r + j, R)
            c = remote(
                go.at[s, :, :, pl.ds(pl.multiple_of(p * oc, oc), oc)],
                ob.at[s, pl.ds(r * G, G)],
                as_.at[s, j],
                ar.at[s, j],
                f,
                p,
            )
            c.start()
            row.append(c)
        turn.append(row)
        c = pltpu.make_async_copy(
            go.at[s, :, :, pl.ds(pl.multiple_of(r * oc, oc), oc)],
            ob.at[s, pl.ds(r * G, G)],
            loc.at[s],
        )
        c.start()
        own.append(c)
    cg = remote(gain, gx, ks.at[0], kr.at[0], partner, r)
    cg.start()
    cross_q = []
    for s in range(2):
        row = []
        for k in range(L):
            j = lax.rem(line + k, L)
            c = remote(gq.at[s, 2 * j + 1 - x], xq.at[s, j], qs.at[s, k], qr.at[s, k], partner, r)
            c.start()
            row.append(c)
        cross_q.append(row)
    back = []
    for s, (src, dst) in enumerate(((dv, rv), (da, ra))):
        for j in range(1, R):
            p = lax.rem(r + j, R)
            c = remote(src.at[p], dst.at[j - 1], ds_.at[s, j], dr.at[s, j], f, p)
            c.start()
            back.append(c)
    cg.wait_recv()
    gb[line] = gain[...] + gx[...]
    line_g = []
    for j in range(1, L):
        c = remote(gb.at[line], gb.at[line], ks.at[j], kr.at[j], lax.rem(line + j, L) * 2 + x, r)
        c.start()
        line_g.append(c)
    cross_o = []
    for s in range(2):
        own[s].wait()
        for c in turn[s]:
            c.wait_recv()
        row = []
        for k in range(L):
            j = lax.rem(line + k, L)
            c = remote(ob.at[s, 2 * j + 1 - x], xo.at[s, j], ps.at[s, k], pr.at[s, k], partner, r)
            c.start()
            row.append(c)
        cross_o.append(row)
    for c in line_g:
        c.wait_recv()
    total = gb[0]
    for j in range(1, L):
        total = total + gb[j]
    gc[r] = total
    group_g = []
    for j in range(1, R):
        c = remote(gc.at[r], gc.at[r], ks.at[L + j], kr.at[L + j], f, lax.rem(r + j, R))
        c.start()
        group_g.append(c)
    along_q = []
    along_o = []
    for s in range(2):
        row_q = []
        row_o = []
        for k in list(range(1, L)) + [0]:
            j = lax.rem(line + k, L)
            cross_q[s][k].wait_recv()
            sq[s, j] = (gq[s, 2 * j + x].astype(f32) + xq[s, j].astype(f32)).astype(bf16)
            if k:
                c = remote(sq.at[s, j], zq.at[s, k - 1], us.at[s, k], ur.at[s, k], 2 * j + x, r)
                c.start()
                row_q.append(c)
            cross_o[s][k].wait_recv()
            so[s, j] = (ob[s, 2 * j + x].astype(f32) + xo[s, j].astype(f32)).astype(bf16)
            if k:
                c = remote(so.at[s, j], zo.at[s, k - 1], vs.at[s, k], vr.at[s, k], 2 * j + x, r)
                c.start()
                row_o.append(c)
        along_q.append(row_q)
        along_o.append(row_o)
    spread = [[], []]
    for s in range(2):
        tq = sq[s, line].astype(f32)
        to = so[s, line].astype(f32)
        for k in range(1, L):
            along_q[s][k - 1].wait_recv()
            tq = tq + zq[s, k - 1].astype(f32)
            along_o[s][k - 1].wait_recv()
            to = to + zo[s, k - 1].astype(f32)
        fb[s, :, pl.ds(0, C3)] = tq.astype(bf16)
        fb[s, :, pl.ds(C3, oc)] = to.astype(bf16)
        fin[s, r, :, pl.ds(0, C3)] = tq.astype(bf16)
        fin[s, r, :, pl.ds(C3, oc)] = to.astype(bf16)
        for j in range(H):
            p = lax.rem(r + 2 * j, R) if j else mate
            c = remote(fb.at[s], fin.at[s, r], es.at[s, j], er.at[s, j], f, p)
            c.start()
            spread[s].append(c)
    last = []
    for s in range(2):
        for j in range(1, H):
            spread[s][j].wait_recv()
            b = lax.rem(r - 2 * j + R, R)
            c = remote(fin.at[s, b], fin.at[s, b], es.at[s, H - 1 + j], er.at[s, H - 1 + j], f, mate)
            c.start()
            last.append(c)
    for c in group_g:
        c.wait_recv()
    total = gc[0]
    for j in range(1, R):
        total = total + gc[j]
    gsum[...] = total
    for c in back + last:
        c.wait()
    for s in range(2):
        spread[s][0].wait_recv()
        for c in spread[s]:
            c.wait_send()
    for c in [cg] + line_g + group_g:
        c.wait_send()
    for s in range(2):
        for c in turn[s] + cross_q[s] + cross_o[s] + along_q[s] + along_o[s]:
            c.wait_send()


def reduce_all(n, R, oc, gq, go, dv, da, gain):
    _, _, rows, C3 = gq.shape
    L = n // 2
    C = C3 + oc
    dma = pltpu.SemaphoreType.DMA
    vm = pl.BlockSpec(memory_space=pltpu.VMEM)
    V = pltpu.VMEM
    return pl.pallas_call(
        functools.partial(reduce_kernel, n, R, oc),
        out_shape=(
            jax.ShapeDtypeStruct((2, R, rows, C), bf16),
            jax.ShapeDtypeStruct((R - 1,) + dv.shape[1:], bf16),
            jax.ShapeDtypeStruct((R - 1,) + da.shape[1:], bf16),
            jax.ShapeDtypeStruct(gain.shape, f32),
        ),
        in_specs=[vm] * 5,
        out_specs=(vm,) * 4,
        scratch_shapes=[
            V((2, n, rows, oc), bf16),
            V((2, L, rows, C3), bf16),
            V((2, L, rows, oc), bf16),
            V((2, L, rows, C3), bf16),
            V((2, L, rows, oc), bf16),
            V((2, L - 1, rows, C3), bf16),
            V((2, L - 1, rows, oc), bf16),
            V((2, rows, C), bf16),
            V(gain.shape, f32),
            V((L,) + gain.shape, f32),
            V((R,) + gain.shape, f32),
            dma((2, R)),
            dma((2, R)),
            dma((2, L)),
            dma((2, L)),
            dma((2, L)),
            dma((2, L)),
            dma((2, L)),
            dma((2, L)),
            dma((2, L)),
            dma((2, L)),
            dma((2, R)),
            dma((2, R)),
            dma((2, R)),
            dma((2, R)),
            dma((L + R,)),
            dma((L + R,)),
            dma((2,)),
        ],
        compiler_params=pltpu.CompilerParams(
            collective_id=1, has_side_effects=True, vmem_limit_bytes=60 * 1024 * 1024
        ),
    )(gq, go, dv, da, gain)


def normalise(z):
    zf = z.astype(f32)
    inverse = lax.rsqrt(jnp.mean(zf * zf, axis=-1, keepdims=True) + 1e-06)
    return zf * inverse, inverse


def mm(a, b, ca, cb):
    return lax.dot_general(a, b, (((ca,), (cb,)), ((), ())), preferred_element_type=f32)


def layer(s, length, gain, wf, wo, got, gq, go, dh, gain_out, hs, qkv_s, dqkv_s, att_s, datt_s, inv_s):
    groups, _, per, P_, D = got.shape
    clips = groups * per
    rows_all = clips * P_
    n, rows = wf.shape[1], wf.shape[2]
    R = wo.shape[1]
    cols = wo.shape[4]
    scale = HEAD ** (-0.5)
    tile = cols
    shards = tile // rows

    def clip_step(c, _):
        z = got[c // per, 0, lax.rem(c, per)].astype(f32)
        inverse = lax.rsqrt(jnp.mean(z * z, axis=1, keepdims=True) + 1e-06)
        at = pl.ds(pl.multiple_of(c * P_, 16), P_)
        inv_s[at, :] = jnp.broadcast_to(inverse, (P_, 128))
        hs[at, :] = (z * inverse * gain[s : s + 1, :]).astype(bf16)
        return 0

    lax.fori_loop(0, clips, clip_step, 0)
    h = hs.at[pl.ds(0, rows_all), :]

    def qkv_step(t, _):
        at = pl.ds(pl.multiple_of(t * cols, 128), cols)
        w = wf[s, :, :, at].reshape(n * rows, cols)
        qkv_s[pl.ds(0, rows_all), at] = mm(h[...], w, 1, 0).astype(bf16)
        return 0

    lax.fori_loop(0, 3, qkv_step, 0)

    total = jnp.zeros((rows_all, cols), f32)
    for k in range(R):
        dy = got[:, 1, :, :, pl.ds(k * cols, cols)].reshape(rows_all, cols)
        total = total + mm(dy, wo[s, k].reshape(cols, cols), 1, 1)
    datt_s[pl.ds(0, rows_all), :] = total.astype(bf16)

    real = lax.broadcasted_iota(jnp.int32, (P_, P_), 1) < length

    def attend(c, _):
        at = pl.ds(pl.multiple_of(c * P_, 16), P_)
        heads = cols // HEAD
        qkv = qkv_s[at, :]
        datt = datt_s[at, :]
        att, dq, dk, dv = [], [], [], []
        for i in range(heads):
            q = qkv[:, i * HEAD : (i + 1) * HEAD]
            k = qkv[:, cols + i * HEAD : cols + (i + 1) * HEAD]
            v = qkv[:, 2 * cols + i * HEAD : 2 * cols + (i + 1) * HEAD]
            da = datt[:, i * HEAD : (i + 1) * HEAD]
            sc = jnp.where(real, mm(q, k, 1, 1) * scale, -1e30)
            e = jnp.exp(sc - jnp.max(sc, axis=1, keepdims=True))
            p = e / jnp.sum(e, axis=1, keepdims=True)
            pb = p.astype(bf16)
            att.append(mm(pb, v, 1, 0).astype(bf16))
            dp = mm(da, v, 1, 1)
            dv.append(mm(pb, da, 0, 0).astype(bf16))
            ds = (p * (dp - jnp.sum(p * dp, axis=1, keepdims=True)) * scale).astype(bf16)
            dq.append(mm(ds, k, 1, 0).astype(bf16))
            dk.append(mm(ds, q, 0, 0).astype(bf16))
        att_s[at, :] = jnp.concatenate(att, 1)
        dqkv_s[at, :] = jnp.concatenate(dq + dk + dv, 1)
        return 0

    lax.fori_loop(0, clips, attend, 0)

    def tile_step(t, _):
        at = pl.ds(pl.multiple_of(t * tile, 128), tile)
        dqkv = dqkv_s[pl.ds(0, rows_all), :]
        dy = got[:, 1, :, :, at].reshape(rows_all, tile)
        out = mm(att_s[pl.ds(0, rows_all), :], dy, 0, 0).astype(bf16)
        go[s, :, :, at] = out.reshape(shards, rows, tile)
        term = mm(h[:, at], dqkv, 0, 0).astype(bf16)
        gq[s, pl.ds(t * shards, shards)] = term.reshape(shards, rows, 3 * cols)
        w = wf[s, pl.ds(t * shards, shards), :, pl.ds(0, 3 * cols)].reshape(tile, 3 * cols)
        d = mm(dqkv, w, 1, 1)
        z = got[:, 0, :, :, at].reshape(rows_all, tile).astype(f32)
        gain_out[s : s + 1, at] = jnp.sum(d * (z * inv_s[pl.ds(0, rows_all), 0:1]), axis=0, keepdims=True)
        dh[:, :, :, at] = d.astype(bf16).reshape(groups, per, P_, tile)
        return 0

    lax.fori_loop(0, D // tile, tile_step, 0)


def layer_scratch(rows_all, D, cols):
    V = pltpu.VMEM
    return [
        V((rows_all, D), bf16),
        V((rows_all, 3 * cols), bf16),
        V((rows_all, 3 * cols), bf16),
        V((rows_all, cols), bf16),
        V((rows_all, cols), bf16),
        V((rows_all, 128), f32),
    ]


def layers_kernel(lengths, wf, wo, gv, ga, gain, gq, go, dv, da, gain_out, *scratch):
    layer(0, lengths[0], gain, wf, wo, gv, gq, go, dv, gain_out, *scratch)
    layer(1, lengths[1], gain, wf, wo, ga, gq, go, da, gain_out, *scratch)


def layers(lengths, wf, wo, gv, ga, gain):
    _, n, rows, C = wf.shape
    _, R, G, _, oc = wo.shape
    D = gv.shape[-1]
    vm = pl.BlockSpec(memory_space=pltpu.VMEM)
    most = max(t.shape[0] * t.shape[2] * t.shape[3] for t in (gv, ga))
    return pl.pallas_call(
        functools.partial(layers_kernel, lengths),
        out_shape=(
            jax.ShapeDtypeStruct((2, n, rows, 3 * oc), bf16),
            jax.ShapeDtypeStruct((2, G, rows, D), bf16),
            jax.ShapeDtypeStruct((R,) + gv.shape[2:], bf16),
            jax.ShapeDtypeStruct((R,) + ga.shape[2:], bf16),
            jax.ShapeDtypeStruct((2, D), f32),
        ),
        in_specs=[vm] * 5,
        out_specs=(vm,) * 5,
        scratch_shapes=layer_scratch(most, D, oc),
        compiler_params=pltpu.CompilerParams(vmem_limit_bytes=60 * 1024 * 1024),
    )(wf, wo, gv, ga, gain)


def d_rows(z, d_out, dh, gain):
    normed, inverse = normalise(z)
    dnorm = dh * gain
    return d_out + inverse * (dnorm - normed * jnp.mean(dnorm * normed, axis=-1, keepdims=True))


def padded(tokens, bottle):
    rows = tokens.shape[1] + bottle.shape[1]
    return jnp.pad(jnp.concatenate([tokens, bottle], 1), ((0, 0), (0, -rows % 16), (0, 0)))


def per_device(
    n,
    R,
    video_in,
    audio_in,
    bottle_in,
    video_gain,
    audio_gain,
    video_qkv,
    video_out,
    audio_qkv,
    audio_out,
    grad_video,
    grad_audio,
    grad_bottle,
):
    r = lax.axis_index("rep")
    clips = video_in.shape[0]
    count = float(clips * n * R)
    rows, width = video_out.shape
    oc = width // R

    def quarter(qkv, out):
        parts = [lax.dynamic_slice_in_dim(qkv, k * width + r * oc, oc, 1) for k in range(3)]
        return jnp.concatenate(parts + [lax.dynamic_slice_in_dim(out, r * oc, oc, 1)], 1)

    w = jnp.stack([quarter(video_qkv, video_out), quarter(audio_qkv, audio_out)])
    half = (grad_bottle.astype(f32) * 0.5).astype(bf16)
    zs = [padded(video_in, bottle_in), padded(audio_in, bottle_in)]
    dys = [padded(grad_video, half), padded(grad_audio, half)]
    tv, ta = [jnp.stack([z, dy]) for z, dy in zip(zs, dys)]
    wf, wo, gv, ga = gather(n, R, oc, w, tv, ta)

    lengths = [t.shape[1] + bottle_in.shape[1] for t in (video_in, audio_in)]
    gains = [video_gain, audio_gain]
    gq, go, dv, da, gain_terms = layers(lengths, wf, wo, gv, ga, jnp.stack(gains))
    dhs = [dv, da]
    fin, rv, ra, gsum = reduce_all(n, R, oc, gq, go, dhs[0], dhs[1], gain_terms)
    gsum = gsum / count

    dzs = []
    for s, got in enumerate((rv, ra)):
        dh = lax.dynamic_index_in_dim(dhs[s], r, 0, keepdims=False).astype(f32)
        for j in range(R - 1):
            dh = dh + got[j].astype(f32)
        dzs.append(d_rows(zs[s], dys[s].astype(f32), dh, gains[s]))
    grads = []
    for s in range(2):
        q = jnp.moveaxis(fin[s, :, :, : 3 * oc].reshape(R, rows, 3, oc), 0, 2)
        grads.append(q.reshape(rows, 3 * width).astype(f32) / count)
        o = jnp.moveaxis(fin[s, :, :, 3 * oc :], 0, 1)
        grads.append(o.reshape(rows, width).astype(f32) / count)
    tv_len, ta_len = video_in.shape[1], audio_in.shape[1]
    dbottle = dzs[0][:, tv_len : lengths[0]] + dzs[1][:, ta_len : lengths[1]]
    return (
        dzs[0][:, :tv_len].astype(bf16),
        dzs[1][:, :ta_len].astype(bf16),
        dbottle.astype(bf16),
        grads[0],
        grads[1],
        grads[2],
        grads[3],
        gsum[0],
        gsum[1],
    )


def solution(mesh):
    n = mesh.shape["fsdp"]
    R = mesh.shape["rep"]
    clip = P(("fsdp", "rep"), None, None)
    shard = P("fsdp", None)
    in_specs = (clip, clip, clip, P(), P(), shard, shard, shard, shard, clip, clip, clip)
    out_specs = (clip, clip, clip, shard, shard, shard, shard, P(), P())
    return jax.shard_map(
        functools.partial(per_device, n, R),
        mesh=mesh,
        in_specs=in_specs,
        out_specs=out_specs,
        check_vma=False,
    )
```

```python
import functools

import jax
import jax.numpy as jnp
from jax import lax
from jax.experimental import pallas as pl
from jax.experimental.pallas import tpu as pltpu
from jax.sharding import PartitionSpec as P

HEAD = 64
f32 = jnp.float32
bf16 = jnp.bfloat16


def remote(src, dst, send, recv, f, r):
    return pltpu.make_async_remote_copy(
        src_ref=src,
        dst_ref=dst,
        send_sem=send,
        recv_sem=recv,
        device_id={"fsdp": f, "rep": r},
        device_id_type=pl.DeviceIdType.MESH,
    )


def places(n, R):
    f = lax.axis_index("fsdp")
    r = lax.axis_index("rep")
    line = f // 2
    x = lax.rem(f, 2)
    return f, r, line, x, f + 1 - 2 * x


def greet(n, R):
    f, r, line, x, partner = places(n, R)
    barrier = pltpu.get_barrier_semaphore()

    def signal(ff, rr):
        pl.semaphore_signal(
            barrier,
            inc=1,
            device_id={"fsdp": ff, "rep": rr},
            device_id_type=pl.DeviceIdType.MESH,
        )

    signal(partner, r)
    for j in range(1, n // 2):
        signal(lax.rem(line + j, n // 2) * 2 + x, r)
    for j in range(1, R):
        signal(f, lax.rem(r + j, R))
    pl.semaphore_wait(barrier, n // 2 + R - 1)


def mm(a, b, ca, cb):
    return lax.dot_general(a, b, (((ca,), (cb,)), ((), ())), preferred_element_type=f32)


def layer(s, length, gain, wf, wo, got, gq, go, dh, gain_out, hs, qkv_s, dqkv_s, att_s, datt_s, inv_s, early, late):
    groups, _, per, P_, D = got.shape
    clips = groups * per
    rows_all = clips * P_
    n, rows = wf.shape[1], wf.shape[2]
    R = wo.shape[1]
    cols = wo.shape[4]
    scale = HEAD ** (-0.5)
    tile = cols
    shards = tile // rows

    def clip_step(c, _):
        z = got[c // per, 0, lax.rem(c, per)].astype(f32)
        inverse = lax.rsqrt(jnp.mean(z * z, axis=1, keepdims=True) + 1e-06)
        at = pl.ds(pl.multiple_of(c * P_, 16), P_)
        inv_s[at, :] = jnp.broadcast_to(inverse, (P_, 128))
        hs[at, :] = (z * inverse * gain[s : s + 1, :]).astype(bf16)
        return 0

    lax.fori_loop(0, clips, clip_step, 0)
    h = hs.at[pl.ds(0, rows_all), :]

    def qkv_step(t, _):
        at = pl.ds(pl.multiple_of(t * cols, 128), cols)
        w = wf[s, :, :, at].reshape(n * rows, cols)
        qkv_s[pl.ds(0, rows_all), at] = mm(h[...], w, 1, 0).astype(bf16)
        return 0

    lax.fori_loop(0, 3, qkv_step, 0)
    early()

    total = jnp.zeros((rows_all, cols), f32)
    for k in range(R):
        dy = got[:, 1, :, :, pl.ds(k * cols, cols)].reshape(rows_all, cols)
        total = total + mm(dy, wo[s, k].reshape(cols, cols), 1, 1)
    datt_s[pl.ds(0, rows_all), :] = total.astype(bf16)

    real = lax.broadcasted_iota(jnp.int32, (P_, P_), 1) < length

    def attend(c, _):
        at = pl.ds(pl.multiple_of(c * P_, 16), P_)
        heads = cols // HEAD
        qkv = qkv_s[at, :]
        datt = datt_s[at, :]
        att, dq, dk, dv = [], [], [], []
        for i in range(heads):
            q = qkv[:, i * HEAD : (i + 1) * HEAD]
            k = qkv[:, cols + i * HEAD : cols + (i + 1) * HEAD]
            v = qkv[:, 2 * cols + i * HEAD : 2 * cols + (i + 1) * HEAD]
            da = datt[:, i * HEAD : (i + 1) * HEAD]
            sc = jnp.where(real, mm(q, k, 1, 1) * scale, -1e30)
            e = jnp.exp(sc - jnp.max(sc, axis=1, keepdims=True))
            p = e / jnp.sum(e, axis=1, keepdims=True)
            pb = p.astype(bf16)
            att.append(mm(pb, v, 1, 0).astype(bf16))
            dp = mm(da, v, 1, 1)
            dv.append(mm(pb, da, 0, 0).astype(bf16))
            ds = (p * (dp - jnp.sum(p * dp, axis=1, keepdims=True)) * scale).astype(bf16)
            dq.append(mm(ds, k, 1, 0).astype(bf16))
            dk.append(mm(ds, q, 0, 0).astype(bf16))
        att_s[at, :] = jnp.concatenate(att, 1)
        dqkv_s[at, :] = jnp.concatenate(dq + dk + dv, 1)
        return 0

    lax.fori_loop(0, clips, attend, 0)
    late()

    def tile_step(t, _):
        at = pl.ds(pl.multiple_of(t * tile, 128), tile)
        dqkv = dqkv_s[pl.ds(0, rows_all), :]
        dy = got[:, 1, :, :, at].reshape(rows_all, tile)
        out = mm(att_s[pl.ds(0, rows_all), :], dy, 0, 0).astype(bf16)
        go[s, :, :, at] = out.reshape(shards, rows, tile)
        term = mm(h[:, at], dqkv, 0, 0).astype(bf16)
        gq[s, pl.ds(t * shards, shards)] = term.reshape(shards, rows, 3 * cols)
        w = wf[s, pl.ds(t * shards, shards), :, pl.ds(0, 3 * cols)].reshape(tile, 3 * cols)
        d = mm(dqkv, w, 1, 1)
        z = got[:, 0, :, :, at].reshape(rows_all, tile).astype(f32)
        gain_out[s : s + 1, at] = jnp.sum(d * (z * inv_s[pl.ds(0, rows_all), 0:1]), axis=0, keepdims=True)
        dh[:, :, :, at] = d.astype(bf16).reshape(groups, per, P_, tile)
        return 0

    lax.fori_loop(0, D // tile, tile_step, 0)


def layer_scratch(rows_all, D, cols):
    V = pltpu.VMEM
    return [
        V((rows_all, D), bf16),
        V((rows_all, 3 * cols), bf16),
        V((rows_all, 3 * cols), bf16),
        V((rows_all, cols), bf16),
        V((rows_all, cols), bf16),
        V((rows_all, 128), f32),
    ]


def kernel(n, R, oc, lengths, count, w_ref, tv_ref, ta_ref, gain_ref,
           dzv, dza, qv, ov, qa, oa, gsum,
           wf, wo, gv, ga, gq, go, dv, da, hs, qkv_s, dqkv_s, att_s, datt_s, inv_s,
           fin, rv, ra, ob, xq, xo, sq, so, zq, zo, fb, gain, gx, gb, gc,
           zs, zr, xs, xr, ts, tr, os, orr,
           as_, ar, qs, qr, ps, pr, us, ur, vs, vr, es, er, ds_, dr, ks, kr, loc):
    L = n // 2
    G = n // R
    H = R // 2
    f, r, line, x, partner = places(n, R)
    mate = r + 1 - 2 * lax.rem(r, 2)
    C = w_ref.shape[2]
    C3 = C - oc
    greet(n, R)
    pending = []

    def go_(c):
        c.start()
        pending.append(c)
        return c

    srcs, gots, dhs, backs = (tv_ref, ta_ref), (gv, ga), (dv, da), (rv, ra)
    own = [pltpu.make_async_copy(w_ref.at[s], wf.at[s, f], loc.at[s]) for s in range(2)]
    own_t = [pltpu.make_async_copy(srcs[s], gots[s].at[r], loc.at[2 + s]) for s in range(2)]
    along, across, tokens, relay = [[], []], [[], []], [[], []], [[], []]
    for s in range(2):
        for j in range(1, L):
            p = lax.rem(line + j, L) * 2 + x
            along[s].append(go_(remote(w_ref.at[s], wf.at[s, f], zs.at[s, j], zr.at[s, j], p, r)))
        across[s].append(go_(remote(w_ref.at[s], wf.at[s, f], xs.at[s, 0], xr.at[s, 0], partner, r)))
        for j in range(1, H):
            p = lax.rem(r + 2 * j, R)
            tokens[s].append(go_(remote(srcs[s], gots[s].at[r], ts.at[s, j], tr.at[s, j], f, p)))
        relay[s].append(go_(remote(srcs[s], gots[s].at[r], ts.at[s, 0], tr.at[s, 0], f, mate)))
    for c in own + own_t:
        c.start()

    def forward(s):
        got = gots[s]
        for j in range(1, L):
            along[s][j - 1].wait_recv()
            b = lax.rem(line - j + L, L) * 2 + x
            across[s].append(go_(remote(wf.at[s, b], wf.at[s, b], xs.at[s, j], xr.at[s, j], partner, r)))
        for j in range(1, H):
            tokens[s][j - 1].wait_recv()
            b = lax.rem(r - 2 * j + R, R)
            k = H - 1 + j
            relay[s].append(go_(remote(got.at[b], got.at[b], ts.at[s, k], tr.at[s, k], f, mate)))

    def exchange_out(s):
        own[s].wait()
        for c in across[s]:
            c.wait_recv()
        swap = []
        for j in range(1, R):
            p = lax.rem(r + j, R)
            src = wf.at[s, pl.ds(p * G, G), :, pl.ds(C3, oc)]
            swap.append(go_(remote(src, wo.at[s, r], os.at[s, j], orr.at[s, j], f, p)))
        c = pltpu.make_async_copy(wf.at[s, pl.ds(r * G, G), :, pl.ds(C3, oc)], wo.at[s, r], loc.at[4 + s])
        c.start()
        own_t[s].wait()
        for k in relay[s]:
            k.wait_recv()
        return swap, c

    def arrived(swap, c):
        c.wait()
        for k in swap:
            k.wait_recv()

    turn, cross_q, cross_o, back = [[], []], [[], []], [[], []], [[], []]
    along_q, along_o, spread, last = [[], []], [[], []], [[], []], [[], []]
    own_o = [
        pltpu.make_async_copy(
            go.at[s, :, :, pl.ds(pl.multiple_of(r * oc, oc), oc)], ob.at[s, pl.ds(r * G, G)], loc.at[6 + s]
        )
        for s in range(2)
    ]

    def reduce_1(s):
        for j in range(1, R):
            p = lax.rem(r + j, R)
            src = go.at[s, :, :, pl.ds(pl.multiple_of(p * oc, oc), oc)]
            turn[s].append(go_(remote(src, ob.at[s, pl.ds(r * G, G)], as_.at[s, j], ar.at[s, j], f, p)))
        own_o[s].start()
        for k in list(range(1, L)) + [0]:
            j = lax.rem(line + k, L)
            c = remote(gq.at[s, 2 * j + 1 - x], xq.at[s, j], qs.at[s, k], qr.at[s, k], partner, r)
            cross_q[s].append(go_(c))
        for j in range(1, R):
            p = lax.rem(r + j, R)
            back[s].append(go_(remote(dhs[s].at[p], backs[s].at[j - 1], ds_.at[s, j], dr.at[s, j], f, p)))

    def reduce_2(s):
        own_o[s].wait()
        for c in turn[s]:
            c.wait_recv()
        for k in list(range(1, L)) + [0]:
            j = lax.rem(line + k, L)
            c = remote(ob.at[s, 2 * j + 1 - x], xo.at[s, j], ps.at[s, k], pr.at[s, k], partner, r)
            cross_o[s].append(go_(c))

    def reduce_3(s):
        for i, k in enumerate(list(range(1, L)) + [0]):
            j = lax.rem(line + k, L)
            cross_q[s][i].wait_recv()
            sq[s, j] = (gq[s, 2 * j + x].astype(f32) + xq[s, j].astype(f32)).astype(bf16)
            if k:
                c = remote(sq.at[s, j], zq.at[s, k - 1], us.at[s, k], ur.at[s, k], 2 * j + x, r)
                along_q[s].append(go_(c))
        for i, k in enumerate(list(range(1, L)) + [0]):
            j = lax.rem(line + k, L)
            cross_o[s][i].wait_recv()
            so[s, j] = (ob[s, 2 * j + x].astype(f32) + xo[s, j].astype(f32)).astype(bf16)
            if k:
                c = remote(so.at[s, j], zo.at[s, k - 1], vs.at[s, k], vr.at[s, k], 2 * j + x, r)
                along_o[s].append(go_(c))

    def reduce_4(s):
        tq = sq[s, line].astype(f32)
        for k in range(1, L):
            along_q[s][k - 1].wait_recv()
            tq = tq + zq[s, k - 1].astype(f32)
        fb[s, :, pl.ds(0, C3)] = tq.astype(bf16)
        to = so[s, line].astype(f32)
        for k in range(1, L):
            along_o[s][k - 1].wait_recv()
            to = to + zo[s, k - 1].astype(f32)
        fb[s, :, pl.ds(C3, oc)] = to.astype(bf16)
        fin[s, r] = fb[s]
        for j in range(H):
            p = lax.rem(r + 2 * j, R) if j else mate
            spread[s].append(go_(remote(fb.at[s], fin.at[s, r], es.at[s, j], er.at[s, j], f, p)))

    def reduce_5(s):
        for j in range(1, H):
            spread[s][j].wait_recv()
            b = lax.rem(r - 2 * j + R, R)
            k = H - 1 + j
            last[s].append(go_(remote(fin.at[s, b], fin.at[s, b], es.at[s, k], er.at[s, k], f, mate)))

    def rows_back(s, dz):
        for c in back[s]:
            c.wait_recv()
        for i in range(dz.shape[0]):
            dh = dhs[s][r, i].astype(f32)
            for j in range(R - 1):
                dh = dh + backs[s][j, i].astype(f32)
            z = srcs[s][0, i].astype(f32)
            inverse = lax.rsqrt(jnp.mean(z * z, axis=1, keepdims=True) + 1e-06)
            normed = z * inverse
            dnorm = dh * gain_ref[s : s + 1, :]
            mean = jnp.mean(dnorm * normed, axis=1, keepdims=True)
            dz[i] = srcs[s][1, i].astype(f32) + inverse * (dnorm - normed * mean)

    def finish(s, q_out, o_out):
        spread[s][0].wait_recv()
        for c in last[s]:
            c.wait_recv()
        width = R * oc
        for g in range(R):
            for k in range(3):
                part = fin[s, g, :, pl.ds(k * oc, oc)].astype(f32) / count
                q_out[:, pl.ds(k * width + g * oc, oc)] = part
            o_out[:, pl.ds(g * oc, oc)] = fin[s, g, :, pl.ds(C3, oc)].astype(f32) / count

    def nothing():
        pass

    work = (hs, qkv_s, dqkv_s, att_s, datt_s, inv_s)
    forward(0)
    arrived(*exchange_out(0))
    layer(0, lengths[0], gain_ref, wf, wo, gv, gq, go, dv, gain, *work, nothing, functools.partial(forward, 1))
    reduce_1(0)
    arrived(*exchange_out(1))
    layer(1, lengths[1], gain_ref, wf, wo, ga, gq, go, da, gain, *work,
          functools.partial(reduce_2, 0), functools.partial(reduce_3, 0))
    reduce_1(1)
    cg = go_(remote(gain, gx, ks.at[0], kr.at[0], partner, r))
    reduce_4(0)
    cg.wait_recv()
    gb[line] = gain[...] + gx[...]
    line_g = []
    for j in range(1, L):
        p = lax.rem(line + j, L) * 2 + x
        line_g.append(go_(remote(gb.at[line], gb.at[line], ks.at[j], kr.at[j], p, r)))
    reduce_2(1)
    rows_back(0, dzv)
    for c in line_g:
        c.wait_recv()
    total = gb[0]
    for j in range(1, L):
        total = total + gb[j]
    gc[r] = total
    group_g = []
    for j in range(1, R):
        p = lax.rem(r + j, R)
        group_g.append(go_(remote(gc.at[r], gc.at[r], ks.at[L + j], kr.at[L + j], f, p)))
    reduce_3(1)
    reduce_5(0)
    rows_back(1, dza)
    for c in group_g:
        c.wait_recv()
    total = gc[0]
    for j in range(1, R):
        total = total + gc[j]
    gsum[...] = total / count
    reduce_4(1)
    finish(0, qv, ov)
    reduce_5(1)
    finish(1, qa, oa)
    for c in pending:
        c.wait_send()


def run(n, R, oc, lengths, count, w, tv, ta, gain):
    _, rows, C = w.shape
    C3 = C - oc
    D = tv.shape[-1]
    L, G, H = n // 2, n // R, R // 2
    dma = pltpu.SemaphoreType.DMA
    V = pltpu.VMEM
    vm = pl.BlockSpec(memory_space=pltpu.VMEM)
    S = jax.ShapeDtypeStruct
    most = max(R * t.shape[1] * t.shape[2] for t in (tv, ta))
    buffers = [
        V((2, n, rows, C), bf16),
        V((2, R, G, rows, oc), bf16),
        V((R,) + tv.shape, bf16),
        V((R,) + ta.shape, bf16),
        V((2, n, rows, C3), bf16),
        V((2, G, rows, D), bf16),
        V((R,) + tv.shape[1:], bf16),
        V((R,) + ta.shape[1:], bf16),
        *layer_scratch(most, D, oc),
        V((2, R, rows, C), bf16),
        V((R - 1,) + tv.shape[1:], bf16),
        V((R - 1,) + ta.shape[1:], bf16),
        V((2, n, rows, oc), bf16),
        V((2, L, rows, C3), bf16),
        V((2, L, rows, oc), bf16),
        V((2, L, rows, C3), bf16),
        V((2, L, rows, oc), bf16),
        V((2, L - 1, rows, C3), bf16),
        V((2, L - 1, rows, oc), bf16),
        V((2, rows, C), bf16),
        V((2, D), f32),
        V((2, D), f32),
        V((L, 2, D), f32),
        V((R, 2, D), f32),
    ]
    sizes = [L, L, 2 * H, R, R, L, L, L, L, R, R]
    sems = []
    for k in sizes:
        sems += [dma((2, k)), dma((2, k))]
    sems += [dma((L + R,)), dma((L + R,)), dma((8,))]
    return pl.pallas_call(
        functools.partial(kernel, n, R, oc, lengths, count),
        out_shape=(
            S(tv.shape[1:], f32),
            S(ta.shape[1:], f32),
            S((rows, 3 * D), f32),
            S((rows, D), f32),
            S((rows, 3 * D), f32),
            S((rows, D), f32),
            S((2, D), f32),
        ),
        in_specs=[vm] * 4,
        out_specs=(vm,) * 7,
        scratch_shapes=buffers + sems,
        compiler_params=pltpu.CompilerParams(
            collective_id=0, has_side_effects=True, vmem_limit_bytes=62 * 1024 * 1024
        ),
    )(w, tv, ta, gain)


def padded(tokens, bottle):
    rows = tokens.shape[1] + bottle.shape[1]
    return jnp.pad(jnp.concatenate([tokens, bottle], 1), ((0, 0), (0, -rows % 16), (0, 0)))


def per_device(
    n,
    R,
    video_in,
    audio_in,
    bottle_in,
    video_gain,
    audio_gain,
    video_qkv,
    video_out,
    audio_qkv,
    audio_out,
    grad_video,
    grad_audio,
    grad_bottle,
):
    r = lax.axis_index("rep")
    clips = video_in.shape[0]
    count = float(clips * n * R)
    rows, width = video_out.shape
    oc = width // R

    def quarter(qkv, out):
        parts = [lax.dynamic_slice_in_dim(qkv, k * width + r * oc, oc, 1) for k in range(3)]
        return jnp.concatenate(parts + [lax.dynamic_slice_in_dim(out, r * oc, oc, 1)], 1)

    w = jnp.stack([quarter(video_qkv, video_out), quarter(audio_qkv, audio_out)])
    half = (grad_bottle.astype(f32) * 0.5).astype(bf16)
    zs = [padded(video_in, bottle_in), padded(audio_in, bottle_in)]
    dys = [padded(grad_video, half), padded(grad_audio, half)]
    tv, ta = [jnp.stack([z, dy]) for z, dy in zip(zs, dys)]
    lengths = [t.shape[1] + bottle_in.shape[1] for t in (video_in, audio_in)]
    gains = jnp.stack([video_gain, audio_gain])
    dzv, dza, qv, ov, qa, oa, gsum = run(n, R, oc, lengths, count, w, tv, ta, gains)
    tv_len, ta_len = video_in.shape[1], audio_in.shape[1]
    dbottle = dzv[:, tv_len : lengths[0]] + dza[:, ta_len : lengths[1]]
    return (
        dzv[:, :tv_len].astype(bf16),
        dza[:, :ta_len].astype(bf16),
        dbottle.astype(bf16),
        qv,
        ov,
        qa,
        oa,
        gsum[0],
        gsum[1],
    )


def solution(mesh):
    n = mesh.shape["fsdp"]
    R = mesh.shape["rep"]
    clip = P(("fsdp", "rep"), None, None)
    shard = P("fsdp", None)
    in_specs = (clip, clip, clip, P(), P(), shard, shard, shard, shard, clip, clip, clip)
    out_specs = (clip, clip, clip, shard, shard, shard, shard, P(), P())
    return jax.shard_map(
        functools.partial(per_device, n, R),
        mesh=mesh,
        in_specs=in_specs,
        out_specs=out_specs,
        check_vma=False,
    )
```

```python
import functools

import jax
import jax.numpy as jnp
from jax import lax
from jax.experimental import pallas as pl
from jax.experimental.pallas import tpu as pltpu
from jax.sharding import PartitionSpec as P

HEAD = 64
f32 = jnp.float32
bf16 = jnp.bfloat16


def remote(src, dst, send, recv, f, r):
    return pltpu.make_async_remote_copy(
        src_ref=src,
        dst_ref=dst,
        send_sem=send,
        recv_sem=recv,
        device_id={"fsdp": f, "rep": r},
        device_id_type=pl.DeviceIdType.MESH,
    )


def places(n, R):
    f = lax.axis_index("fsdp")
    r = lax.axis_index("rep")
    line = f // 2
    x = lax.rem(f, 2)
    return f, r, line, x, f + 1 - 2 * x


def greet(n, R):
    f, r, line, x, partner = places(n, R)
    barrier = pltpu.get_barrier_semaphore()

    def signal(ff, rr):
        pl.semaphore_signal(
            barrier,
            inc=1,
            device_id={"fsdp": ff, "rep": rr},
            device_id_type=pl.DeviceIdType.MESH,
        )

    signal(partner, r)
    for j in range(1, n // 2):
        signal(lax.rem(line + j, n // 2) * 2 + x, r)
    for j in range(1, R):
        signal(f, lax.rem(r + j, R))
    pl.semaphore_wait(barrier, n // 2 + R - 1)


def mm(a, b, ca, cb):
    return lax.dot_general(a, b, (((ca,), (cb,)), ((), ())), preferred_element_type=f32)


def layer(s, length, gain, wf, wo, got, gq, go, dh, gain_out, hs, qkv_s, dqkv_s, att_s, datt_s, inv_s, early, late):
    groups, _, per, P_, D = got.shape
    clips = groups * per
    rows_all = clips * P_
    n, rows = wf.shape[1], wf.shape[2]
    R = wo.shape[1]
    cols = wo.shape[4]
    scale = HEAD ** (-0.5)
    tile = cols
    shards = tile // rows

    def clip_step(c, _):
        z = got[c // per, 0, lax.rem(c, per)].astype(f32)
        inverse = lax.rsqrt(jnp.mean(z * z, axis=1, keepdims=True) + 1e-06)
        at = pl.ds(pl.multiple_of(c * P_, 16), P_)
        inv_s[at, :] = jnp.broadcast_to(inverse, (P_, 128))
        hs[at, :] = (z * inverse * gain[s : s + 1, :]).astype(bf16)
        return 0

    lax.fori_loop(0, clips, clip_step, 0)
    h = hs.at[pl.ds(0, rows_all), :]

    def qkv_step(t, _):
        at = pl.ds(pl.multiple_of(t * cols, 128), cols)
        w = wf[s, :, :, at].reshape(n * rows, cols)
        qkv_s[pl.ds(0, rows_all), at] = mm(h[...], w, 1, 0).astype(bf16)
        return 0

    lax.fori_loop(0, 3, qkv_step, 0)
    early()

    total = jnp.zeros((rows_all, cols), f32)
    for k in range(R):
        dy = got[:, 1, :, :, pl.ds(k * cols, cols)].reshape(rows_all, cols)
        total = total + mm(dy, wo[s, k].reshape(cols, cols), 1, 1)
    datt_s[pl.ds(0, rows_all), :] = total.astype(bf16)

    real = lax.broadcasted_iota(jnp.int32, (P_, P_), 1) < length

    def attend(c, _):
        at = pl.ds(pl.multiple_of(c * P_, 16), P_)
        heads = cols // HEAD
        qkv = qkv_s[at, :]
        datt = datt_s[at, :]
        att, dq, dk, dv = [], [], [], []
        for i in range(heads):
            q = qkv[:, i * HEAD : (i + 1) * HEAD]
            k = qkv[:, cols + i * HEAD : cols + (i + 1) * HEAD]
            v = qkv[:, 2 * cols + i * HEAD : 2 * cols + (i + 1) * HEAD]
            da = datt[:, i * HEAD : (i + 1) * HEAD]
            sc = jnp.where(real, mm(q, k, 1, 1) * scale, -1e30)
            e = jnp.exp(sc - jnp.max(sc, axis=1, keepdims=True))
            p = e / jnp.sum(e, axis=1, keepdims=True)
            pb = p.astype(bf16)
            att.append(mm(pb, v, 1, 0).astype(bf16))
            dp = mm(da, v, 1, 1)
            dv.append(mm(pb, da, 0, 0).astype(bf16))
            ds = (p * (dp - jnp.sum(p * dp, axis=1, keepdims=True)) * scale).astype(bf16)
            dq.append(mm(ds, k, 1, 0).astype(bf16))
            dk.append(mm(ds, q, 0, 0).astype(bf16))
        att_s[at, :] = jnp.concatenate(att, 1)
        dqkv_s[at, :] = jnp.concatenate(dq + dk + dv, 1)
        return 0

    lax.fori_loop(0, clips, attend, 0)
    late()

    def tile_step(t, _):
        at = pl.ds(pl.multiple_of(t * tile, 128), tile)
        dqkv = dqkv_s[pl.ds(0, rows_all), :]
        dy = got[:, 1, :, :, at].reshape(rows_all, tile)
        out = mm(att_s[pl.ds(0, rows_all), :], dy, 0, 0).astype(bf16)
        go[s, :, :, at] = out.reshape(shards, rows, tile)
        term = mm(h[:, at], dqkv, 0, 0).astype(bf16)
        gq[s, pl.ds(t * shards, shards)] = term.reshape(shards, rows, 3 * cols)
        w = wf[s, pl.ds(t * shards, shards), :, pl.ds(0, 3 * cols)].reshape(tile, 3 * cols)
        d = mm(dqkv, w, 1, 1)
        z = got[:, 0, :, :, at].reshape(rows_all, tile).astype(f32)
        gain_out[s : s + 1, at] = jnp.sum(d * (z * inv_s[pl.ds(0, rows_all), 0:1]), axis=0, keepdims=True)
        dh[:, :, :, at] = d.astype(bf16).reshape(groups, per, P_, tile)
        return 0

    lax.fori_loop(0, D // tile, tile_step, 0)


def layer_scratch(rows_all, D, cols):
    V = pltpu.VMEM
    return [
        V((rows_all, D), bf16),
        V((rows_all, 3 * cols), bf16),
        V((rows_all, 3 * cols), bf16),
        V((rows_all, cols), bf16),
        V((rows_all, cols), bf16),
        V((rows_all, 128), f32),
    ]


def kernel(n, R, oc, lengths, count, w_ref, tv_ref, ta_ref, gain_ref,
           dzv, dza, dzb, qv, ov, qa, oa, gsum,
           wf, wo, gv, ga, gq, go, dv, da, hs, qkv_s, dqkv_s, att_s, datt_s, inv_s,
           fin, rv, ra, ob, xq, xo, sq, so, zq, zo, fb, gain, gx, gb, gc,
           zs, zr, xs, xr, ts, tr, os, orr,
           as_, ar, qs, qr, ps, pr, us, ur, vs, vr, es, er, ds_, dr, ks, kr, loc):
    L = n // 2
    G = n // R
    H = R // 2
    f, r, line, x, partner = places(n, R)
    mate = r + 1 - 2 * lax.rem(r, 2)
    C = w_ref.shape[2]
    C3 = C - oc
    greet(n, R)
    pending = []

    def go_(c):
        c.start()
        pending.append(c)
        return c

    srcs, gots, dhs, backs = (tv_ref, ta_ref), (gv, ga), (dv, da), (rv, ra)
    own = [pltpu.make_async_copy(w_ref.at[s], wf.at[s, f], loc.at[s]) for s in range(2)]
    own_t = [pltpu.make_async_copy(srcs[s], gots[s].at[r], loc.at[2 + s]) for s in range(2)]
    along, across, tokens, relay = [[], []], [[], []], [[], []], [[], []]

    def own_across(s):
        c = remote(w_ref.at[s], wf.at[s, f], xs.at[s, 0], xr.at[s, 0], partner, r)
        across[s].append(go_(c))

    for s in range(2):
        for j in range(1, L):
            p = lax.rem(line + j, L) * 2 + x
            along[s].append(go_(remote(w_ref.at[s], wf.at[s, f], zs.at[s, j], zr.at[s, j], p, r)))
        if s == 0:
            own_across(s)
        for j in range(1, H):
            p = lax.rem(r + 2 * j, R)
            tokens[s].append(go_(remote(srcs[s], gots[s].at[r], ts.at[s, j], tr.at[s, j], f, p)))
        relay[s].append(go_(remote(srcs[s], gots[s].at[r], ts.at[s, 0], tr.at[s, 0], f, mate)))
    for c in own + own_t:
        c.start()

    def forward(s):
        got = gots[s]
        for j in range(1, L):
            along[s][j - 1].wait_recv()
            b = lax.rem(line - j + L, L) * 2 + x
            across[s].append(go_(remote(wf.at[s, b], wf.at[s, b], xs.at[s, j], xr.at[s, j], partner, r)))
        for j in range(1, H):
            tokens[s][j - 1].wait_recv()
            b = lax.rem(r - 2 * j + R, R)
            k = H - 1 + j
            relay[s].append(go_(remote(got.at[b], got.at[b], ts.at[s, k], tr.at[s, k], f, mate)))

    def exchange_out(s):
        own[s].wait()
        for c in across[s]:
            c.wait_recv()
        swap = []
        for j in range(1, R):
            p = lax.rem(r + j, R)
            src = wf.at[s, pl.ds(p * G, G), :, pl.ds(C3, oc)]
            swap.append(go_(remote(src, wo.at[s, r], os.at[s, j], orr.at[s, j], f, p)))
        c = pltpu.make_async_copy(wf.at[s, pl.ds(r * G, G), :, pl.ds(C3, oc)], wo.at[s, r], loc.at[4 + s])
        c.start()
        own_t[s].wait()
        for k in relay[s]:
            k.wait_recv()
        return swap, c

    def arrived(swap, c):
        c.wait()
        for k in swap:
            k.wait_recv()

    turn, cross_q, cross_o, back = [[], []], [[], []], [[], []], [[], []]
    along_q, along_o, spread, last = [[], []], [[], []], [[], []], [[], []]
    own_o = [
        pltpu.make_async_copy(
            go.at[s, :, :, pl.ds(pl.multiple_of(r * oc, oc), oc)], ob.at[s, pl.ds(r * G, G)], loc.at[6 + s]
        )
        for s in range(2)
    ]

    def reduce_1(s):
        for j in range(1, R):
            p = lax.rem(r + j, R)
            src = go.at[s, :, :, pl.ds(pl.multiple_of(p * oc, oc), oc)]
            turn[s].append(go_(remote(src, ob.at[s, pl.ds(r * G, G)], as_.at[s, j], ar.at[s, j], f, p)))
        own_o[s].start()
        for k in list(range(1, L)) + [0]:
            j = lax.rem(line + k, L)
            c = remote(gq.at[s, 2 * j + 1 - x], xq.at[s, j], qs.at[s, k], qr.at[s, k], partner, r)
            cross_q[s].append(go_(c))
        for j in range(1, R):
            p = lax.rem(r + j, R)
            back[s].append(go_(remote(dhs[s].at[p], backs[s].at[j - 1], ds_.at[s, j], dr.at[s, j], f, p)))

    def reduce_2(s):
        own_o[s].wait()
        for c in turn[s]:
            c.wait_recv()
        for k in list(range(1, L)) + [0]:
            j = lax.rem(line + k, L)
            c = remote(ob.at[s, 2 * j + 1 - x], xo.at[s, j], ps.at[s, k], pr.at[s, k], partner, r)
            cross_o[s].append(go_(c))

    def reduce_3(s):
        for i, k in enumerate(list(range(1, L)) + [0]):
            j = lax.rem(line + k, L)
            cross_q[s][i].wait_recv()
            sq[s, j] = (gq[s, 2 * j + x].astype(f32) + xq[s, j].astype(f32)).astype(bf16)
            if k:
                c = remote(sq.at[s, j], zq.at[s, k - 1], us.at[s, k], ur.at[s, k], 2 * j + x, r)
                along_q[s].append(go_(c))
        for i, k in enumerate(list(range(1, L)) + [0]):
            j = lax.rem(line + k, L)
            cross_o[s][i].wait_recv()
            so[s, j] = (ob[s, 2 * j + x].astype(f32) + xo[s, j].astype(f32)).astype(bf16)
            if k:
                c = remote(so.at[s, j], zo.at[s, k - 1], vs.at[s, k], vr.at[s, k], 2 * j + x, r)
                along_o[s].append(go_(c))

    def reduce_4(s):
        tq = sq[s, line].astype(f32)
        for k in range(1, L):
            along_q[s][k - 1].wait_recv()
            tq = tq + zq[s, k - 1].astype(f32)
        fb[s, :, pl.ds(0, C3)] = tq.astype(bf16)
        to = so[s, line].astype(f32)
        for k in range(1, L):
            along_o[s][k - 1].wait_recv()
            to = to + zo[s, k - 1].astype(f32)
        fb[s, :, pl.ds(C3, oc)] = to.astype(bf16)
        fin[s, r] = fb[s]
        for j in range(H):
            p = lax.rem(r + 2 * j, R) if j else mate
            spread[s].append(go_(remote(fb.at[s], fin.at[s, r], es.at[s, j], er.at[s, j], f, p)))

    def reduce_5(s):
        for j in range(1, H):
            spread[s][j].wait_recv()
            b = lax.rem(r - 2 * j + R, R)
            k = H - 1 + j
            last[s].append(go_(remote(fin.at[s, b], fin.at[s, b], es.at[s, k], er.at[s, k], f, mate)))

    def rows_back(s, out):
        own_rows = out.shape[1]
        nb = lengths[s] - own_rows
        for c in back[s]:
            c.wait_recv()
        for i in range(out.shape[0]):
            dh = dhs[s][r, i].astype(f32)
            for j in range(R - 1):
                dh = dh + backs[s][j, i].astype(f32)
            z = srcs[s][0, i].astype(f32)
            inverse = lax.rsqrt(jnp.mean(z * z, axis=1, keepdims=True) + 1e-06)
            normed = z * inverse
            dnorm = dh * gain_ref[s : s + 1, :]
            mean = jnp.mean(dnorm * normed, axis=1, keepdims=True)
            dz = srcs[s][1, i].astype(f32) + inverse * (dnorm - normed * mean)
            out[i] = dz[:own_rows].astype(bf16)
            dzb[s, i] = dz[own_rows : own_rows + nb]

    def finish(s, q_out, o_out):
        spread[s][0].wait_recv()
        for c in last[s]:
            c.wait_recv()
        width = R * oc
        for g in range(R):
            for k in range(3):
                part = fin[s, g, :, pl.ds(k * oc, oc)].astype(f32) / count
                q_out[:, pl.ds(k * width + g * oc, oc)] = part
            o_out[:, pl.ds(g * oc, oc)] = fin[s, g, :, pl.ds(C3, oc)].astype(f32) / count

    def nothing():
        pass

    work = (hs, qkv_s, dqkv_s, att_s, datt_s, inv_s)
    forward(0)
    own_across(1)
    swap_0 = exchange_out(0)

    def early_0():
        arrived(*swap_0)
        forward(1)

    layer(0, lengths[0], gain_ref, wf, wo, gv, gq, go, dv, gain, *work, early_0, nothing)
    reduce_1(0)
    swap_1 = exchange_out(1)

    def early_1():
        arrived(*swap_1)
        reduce_2(0)

    layer(1, lengths[1], gain_ref, wf, wo, ga, gq, go, da, gain, *work,
          early_1, functools.partial(reduce_3, 0))
    reduce_1(1)
    cg = go_(remote(gain, gx, ks.at[0], kr.at[0], partner, r))
    reduce_4(0)
    cg.wait_recv()
    gb[line] = gain[...] + gx[...]
    line_g = []
    for j in range(1, L):
        p = lax.rem(line + j, L) * 2 + x
        line_g.append(go_(remote(gb.at[line], gb.at[line], ks.at[j], kr.at[j], p, r)))
    reduce_2(1)
    rows_back(0, dzv)
    for c in line_g:
        c.wait_recv()
    total = gb[0]
    for j in range(1, L):
        total = total + gb[j]
    gc[r] = total
    group_g = []
    for j in range(1, R):
        p = lax.rem(r + j, R)
        group_g.append(go_(remote(gc.at[r], gc.at[r], ks.at[L + j], kr.at[L + j], f, p)))
    reduce_3(1)
    reduce_5(0)
    rows_back(1, dza)
    for c in group_g:
        c.wait_recv()
    total = gc[0]
    for j in range(1, R):
        total = total + gc[j]
    gsum[...] = total / count
    reduce_4(1)
    finish(0, qv, ov)
    reduce_5(1)
    finish(1, qa, oa)
    for c in pending:
        c.wait_send()


def run(n, R, oc, lengths, own_rows, count, w, tv, ta, gain):
    _, rows, C = w.shape
    C3 = C - oc
    D = tv.shape[-1]
    L, G, H = n // 2, n // R, R // 2
    dma = pltpu.SemaphoreType.DMA
    V = pltpu.VMEM
    vm = pl.BlockSpec(memory_space=pltpu.VMEM)
    S = jax.ShapeDtypeStruct
    clips = tv.shape[1]
    most = max(R * t.shape[1] * t.shape[2] for t in (tv, ta))
    buffers = [
        V((2, n, rows, C), bf16),
        V((2, R, G, rows, oc), bf16),
        V((R,) + tv.shape, bf16),
        V((R,) + ta.shape, bf16),
        V((2, n, rows, C3), bf16),
        V((2, G, rows, D), bf16),
        V((R,) + tv.shape[1:], bf16),
        V((R,) + ta.shape[1:], bf16),
        *layer_scratch(most, D, oc),
        V((2, R, rows, C), bf16),
        V((R - 1,) + tv.shape[1:], bf16),
        V((R - 1,) + ta.shape[1:], bf16),
        V((2, n, rows, oc), bf16),
        V((2, L, rows, C3), bf16),
        V((2, L, rows, oc), bf16),
        V((2, L, rows, C3), bf16),
        V((2, L, rows, oc), bf16),
        V((2, L - 1, rows, C3), bf16),
        V((2, L - 1, rows, oc), bf16),
        V((2, rows, C), bf16),
        V((2, D), f32),
        V((2, D), f32),
        V((L, 2, D), f32),
        V((R, 2, D), f32),
    ]
    sizes = [L, L, 2 * H, R, R, L, L, L, L, R, R]
    sems = []
    for k in sizes:
        sems += [dma((2, k)), dma((2, k))]
    sems += [dma((L + R,)), dma((L + R,)), dma((8,))]
    return pl.pallas_call(
        functools.partial(kernel, n, R, oc, lengths, count),
        out_shape=(
            *(S((clips, t, D), bf16) for t in own_rows),
            S((2, clips, lengths[0] - own_rows[0], D), f32),
            S((rows, 3 * D), f32),
            S((rows, D), f32),
            S((rows, 3 * D), f32),
            S((rows, D), f32),
            S((2, D), f32),
        ),
        in_specs=[vm] * 4,
        out_specs=(vm,) * 8,
        scratch_shapes=buffers + sems,
        compiler_params=pltpu.CompilerParams(
            collective_id=0, has_side_effects=True, vmem_limit_bytes=62 * 1024 * 1024
        ),
    )(w, tv, ta, gain)


def padded(tokens, bottle):
    rows = tokens.shape[1] + bottle.shape[1]
    return jnp.pad(jnp.concatenate([tokens, bottle], 1), ((0, 0), (0, -rows % 16), (0, 0)))


def per_device(
    n,
    R,
    video_in,
    audio_in,
    bottle_in,
    video_gain,
    audio_gain,
    video_qkv,
    video_out,
    audio_qkv,
    audio_out,
    grad_video,
    grad_audio,
    grad_bottle,
):
    r = lax.axis_index("rep")
    clips = video_in.shape[0]
    count = float(clips * n * R)
    rows, width = video_out.shape
    oc = width // R

    def quarter(qkv, out):
        parts = [lax.dynamic_slice_in_dim(qkv, k * width + r * oc, oc, 1) for k in range(3)]
        return jnp.concatenate(parts + [lax.dynamic_slice_in_dim(out, r * oc, oc, 1)], 1)

    w = jnp.stack([quarter(video_qkv, video_out), quarter(audio_qkv, audio_out)])
    half = (grad_bottle.astype(f32) * 0.5).astype(bf16)
    zs = [padded(video_in, bottle_in), padded(audio_in, bottle_in)]
    dys = [padded(grad_video, half), padded(grad_audio, half)]
    tv, ta = [jnp.stack([z, dy]) for z, dy in zip(zs, dys)]
    lengths = [t.shape[1] + bottle_in.shape[1] for t in (video_in, audio_in)]
    gains = jnp.stack([video_gain, audio_gain])
    own_rows = (video_in.shape[1], audio_in.shape[1])
    dzv, dza, dzb, qv, ov, qa, oa, gsum = run(n, R, oc, lengths, own_rows, count, w, tv, ta, gains)
    return (
        dzv,
        dza,
        (dzb[0] + dzb[1]).astype(bf16),
        qv,
        ov,
        qa,
        oa,
        gsum[0],
        gsum[1],
    )


def solution(mesh):
    n = mesh.shape["fsdp"]
    R = mesh.shape["rep"]
    clip = P(("fsdp", "rep"), None, None)
    shard = P("fsdp", None)
    in_specs = (clip, clip, clip, P(), P(), shard, shard, shard, shard, clip, clip, clip)
    out_specs = (clip, clip, clip, shard, shard, shard, shard, P(), P())
    return jax.shard_map(
        functools.partial(per_device, n, R),
        mesh=mesh,
        in_specs=in_specs,
        out_specs=out_specs,
        check_vma=False,
    )
```
